32 devices in a mesh: dp: 4 (over z), blk: 4 (over x, core), uly: 2 (over y).
Axes of the slice: x: 2, y: 2, z: 4, core: 2. Of those that a mesh axis runs over, the one named last changes fastest.
Arguments:
- query_act: bfloat16 [4, 512, 2048], P('dp', ('blk', 'uly')), may hold values from -8.7 to 8.7
- key_act: bfloat16 [4, 512, 512], P('dp', ('blk', 'uly')), may hold values from -8.7 to 8.7
- value_act: bfloat16 [4, 512, 512], P('dp', ('blk', 'uly')), may hold values from -6 to 6
- out_grad: bfloat16 [4, 512, 2048], P('dp', ('blk', 'uly')), may hold values from -4 to 4
- layer_input: bfloat16 [4, 512, 3072], P('dp', 'blk'), may hold values from -5 to 5
- segments: int32 [4, 512], P('dp'), may hold values from 0 to 3, never falling along the last dimension, each value on 1 to 256 neighbouring positions
- allow_table: int32 [4, 4, 4], P('dp', 'blk'), may hold values from 0 to 1, as said below
Outputs:
- query_grad: bfloat16 [4, 512, 2048], P('dp', 'blk', 'uly')
- key_grad: bfloat16 [4, 512, 512], P('dp', 'blk', 'uly')
- value_grad: bfloat16 [4, 512, 512], P('dp', 'blk', 'uly')
- weight_grad: float32 [3072, 512], P(('dp', 'blk'), 'uly')
The draws below stay inside these ranges and needn't reach their ends.
Inputs may be any that keep to these rules, and one draw needn't show every extreme that they name: allow_table[d, i, 0] is 1: every query block takes keys from its own block.
All inputs are finite; a program needn't handle non-finite values.
Results may differ from the reference program's by a relative error of at most 0.0096.
Values may be sent and summed in bfloat16 or wider, within the bound.
A program may use at most 64 MiB of HBM per device.

```python
import math
import jax
import jax.numpy as jnp
import numpy as np
from jax import lax

DH = 128
GROUP = 4
KVH = 4
QH = 16
DIN = 3072
BLK_ROWS = 128
DOC_COUNT = 4
BLOCKS = 4
WINDOW = 512
DOCS = 4
TOKENS = 2048


def paired_draw(key):
    query_key = jax.random.fold_in(key, 101)
    key_key = jax.random.fold_in(key, 202)
    queries = jnp.clip(jax.random.normal(query_key, (TOKENS, QH * DH), jnp.float32), -4.0, 4.0)
    keyed = jnp.clip(jax.random.normal(key_key, (TOKENS, KVH * DH), jnp.float32), -4.0, 4.0)
    return (queries.reshape(DOCS, WINDOW, QH * DH), keyed.reshape(DOCS, WINDOW, KVH * DH))


def draw_query_act(key, part):
    return paired_draw(key)[0].astype(jnp.bfloat16)


def draw_key_act(key, part):
    return paired_draw(key)[1].astype(jnp.bfloat16)


def draw_allow_table(key, part):
    bits = jax.random.randint(jax.random.fold_in(key, 404), (DOCS, BLOCKS, BLOCKS), 0, 2, dtype=jnp.int32)
    first = jnp.arange(BLOCKS, dtype=jnp.int32)[None, None, :] == 0
    return jnp.where(first, 1, bits).astype(jnp.int32)


def strengthened(entries, key, source, target, shards_of, factor):
    def block_of(axis_at):
        return (jnp.arange(entries.shape[axis_at]) // (entries.shape[axis_at] // shards_of)).reshape((-1,) + (1,) * (entries.ndim - 1 - axis_at))

    near = jax.random.permutation(key, shards_of)[block_of(target)]
    other_side = (block_of(target) + shards_of // 2) % shards_of
    return jnp.where((block_of(source) == near) | (block_of(source) == other_side), factor * entries, entries)


def levels(own_key, extent, split, smallest, top_value):
    loudness, own = 1.0, jax.random.fold_in(own_key, 6)
    for dim, blocks in split:
        draws = jnp.exp(jax.random.uniform(jax.random.fold_in(own, dim), (blocks,), jnp.float32, smallest / len(split), top_value / len(split)))
        loudness = loudness * jnp.repeat(draws, extent[dim] // blocks).reshape([-1 if axis == dim else 1 for axis in range(len(extent))])
    return loudness


def split_up(count, total, most, lean):
    weights = [(1 << 20) // math.isqrt(grade ** lean) + 1 for grade in range(2, count + 1)]
    surplus, holding = total - most - (count - 1), [1] * (count - 1)
    while surplus > 0:
        candidates = [i for i in range(count - 1) if holding[i] < most]
        mass, remaining = sum([weights[i] for i in candidates]), surplus
        for i in candidates:
            addition = min(most - holding[i], max(1, remaining * weights[i] // mass), surplus)
            holding[i] = holding[i] + addition
            surplus = surplus - addition
    return np.array([most] + holding)


def ragged(rng, number_of, total, most, lean):
    if number_of == 2:
        one = jax.random.randint(rng, (), max(1, total - most), min(most, total - 1) + 1)
        return jnp.stack([one, total - one])
    lengths = jnp.asarray(split_up(number_of, total, most, lean), jnp.int32)
    couples = (number_of - 1) // 2
    source_of, receiver = lengths[1:1 + 2 * couples:2], lengths[2:2 + 2 * couples:2]
    slack = jnp.minimum(source_of - 1, most - receiver)
    passed = jax.random.randint(jax.random.fold_in(rng, 1), (couples,), 0, 1 << 20) % (slack + 1)
    lengths = lengths.at[1:1 + 2 * couples:2].set(source_of - passed).at[2:2 + 2 * couples:2].set(receiver + passed)
    return lengths[jax.random.permutation(jax.random.fold_in(rng, 2), number_of)]


def normal_values(key, dims, scale, bound, shards=(), kind=jnp.bfloat16):
    gain = levels(key, dims, shards, -0.22, 0.18) if shards else 1.0
    result = jax.random.normal(key, dims, jnp.float32) * scale * gain
    return jnp.minimum(jnp.maximum(result, -bound), bound).astype(kind)


def gaussian_with(own_key, dims, deviation, bound, pieces, heavy, kind=jnp.bfloat16):
    values = deviation * jax.random.normal(own_key, dims, jnp.float32)
    if pieces:
        values = values * levels(own_key, dims, pieces, -0.22, 0.18)
    return jnp.clip(strengthened(values, jax.random.fold_in(own_key, 3), *heavy), -bound, bound).astype(kind)


def setup_inputs(seed: int = 0) -> dict:
    seeds = jax.random.split(jax.random.key(seed), 8)
    return {
        "query_act": draw_query_act(jax.random.fold_in(seeds[7], 71), 0),
        "key_act": draw_key_act(jax.random.fold_in(seeds[7], 71), 0),
        "value_act": normal_values(seeds[2], (DOCS, WINDOW, KVH * DH), 1.0, 6.0, ((0, 4), (1, 8))),
        "out_grad": normal_values(seeds[3], (DOCS, WINDOW, QH * DH), 0.3, 4.0, ((0, 4), (1, 8))),
        "layer_input": gaussian_with(seeds[4], (DOCS, WINDOW, DIN), 0.25, 5.0, ((0, 4), (1, 4)), (0, 2, 4, 2.0)),
        "segments": jax.vmap(lambda own: jnp.searchsorted(jnp.cumsum(ragged(own, DOC_COUNT, WINDOW, WINDOW // 2, 0)), jnp.arange(WINDOW), side="right"))(jax.random.split(seeds[5], DOCS)).reshape((DOCS, WINDOW)).astype(jnp.int32),
        "allow_table": draw_allow_table(jax.random.fold_in(seeds[7], 71), 0),
    }


NEG_FILL = -1.0e30
HIGH = lax.Precision.HIGHEST


def rounded(value):
    return lax.optimization_barrier(value.astype(jnp.bfloat16)).astype(jnp.float32)


def reference(query_act, key_act, value_act, out_grad, layer_input, segments, allow_table):
    score_scale = DH ** -0.5
    positions = jnp.arange(WINDOW, dtype=jnp.int32)
    block_ids = positions // BLK_ROWS
    step_ids = (block_ids[:, None] - block_ids[None, :]) % BLOCKS
    causal = positions[None, :] <= positions[:, None]

    def one_window(total, item):
        query_doc, key_doc, value_doc, grad_doc, input_doc, segment_doc, table_doc = item
        query_four = query_doc.astype(jnp.float32).reshape(WINDOW, KVH, GROUP, DH)
        grad_four = grad_doc.astype(jnp.float32).reshape(WINDOW, KVH, GROUP, DH)
        key_three = key_doc.astype(jnp.float32).reshape(WINDOW, KVH, DH)
        value_three = value_doc.astype(jnp.float32).reshape(WINDOW, KVH, DH)
        allowed = table_doc[block_ids[:, None], step_ids] == 1
        visible = causal & (segment_doc[None, :] == segment_doc[:, None]) & allowed
        scores = jnp.einsum("qhgd,khd->hgqk", query_four, key_three, precision=HIGH) * score_scale
        peak = jnp.max(jnp.where(visible, scores, NEG_FILL), axis=-1)
        shifted = jnp.where(visible, jnp.exp(scores - peak[..., None]), 0.0)
        log_total = peak + jnp.log(jnp.sum(shifted, axis=-1))
        probs = jnp.where(visible, jnp.exp(scores - log_total[..., None]), 0.0)
        probs_low = rounded(probs)
        attended = jnp.einsum("hgqk,khd->hgqd", probs_low, value_three, precision=HIGH)
        row_delta = jnp.einsum("qhgd,hgqd->hgq", grad_four, attended, precision=HIGH)
        prob_grad = jnp.einsum("qhgd,khd->hgqk", grad_four, value_three, precision=HIGH)
        score_grad = rounded(probs * (prob_grad - row_delta[..., None]))
        query_grad = jnp.einsum("hgqk,khd->qhgd", score_grad, key_three, precision=HIGH) * score_scale
        key_grad = jnp.einsum("hgqk,qhgd->khd", score_grad, query_four, precision=HIGH) * score_scale
        value_grad = jnp.einsum("hgqk,qhgd->khd", probs_low, grad_four, precision=HIGH)
        value_low = value_grad.reshape(WINDOW, KVH * DH).astype(jnp.bfloat16)
        total = total + jnp.dot(input_doc.T, value_low, preferred_element_type=jnp.float32)
        outputs = (query_grad.reshape(WINDOW, QH * DH).astype(jnp.bfloat16),
                   key_grad.reshape(WINDOW, KVH * DH).astype(jnp.bfloat16),
                   value_low)
        return total, outputs

    items = (query_act, key_act, value_act, out_grad, layer_input, segments, allow_table)
    start = jnp.zeros((DIN, KVH * DH), jnp.float32)
    weight_grad, stacked = lax.scan(one_window, start, items)
    return (stacked[0], stacked[1], stacked[2], weight_grad)
```

```python
import functools

import jax
import jax.numpy as jnp
from jax import lax
from jax.experimental import pallas as pl
from jax.experimental.pallas import tpu as pltpu
from jax.sharding import PartitionSpec as P

DH = 128
GROUP = 4
MESH = pl.DeviceIdType.MESH
NEG = -1e30
CUT = None


def dot(a, b, ca, cb):
    return lax.dot_general(a, b, (((ca,), (cb,)), ((), ())), preferred_element_type=jnp.float32)


def guarded(cond, run):
    if cond is None:
        run()
    else:
        pl.when(cond)(run)


class Send:
    def __init__(self, cp, goes, comes):
        self.cp, self.goes, self.comes = cp, goes, comes
        self.started, self.landed = False, False

    def start(self):
        self.started = True
        guarded(self.goes, self.cp.start)

    def wait_recv(self):
        if self.started and not self.landed:
            self.landed = True
            guarded(self.comes, self.cp.wait_recv)

    def finish(self):
        if self.started:
            self.wait_recv()
            guarded(self.goes, self.cp.wait_send)


def kernel(cut, *args):
    sends = []
    for name in stages(sends, *args):
        if name == cut:
            break
    for cp in sends:
        cp.finish()


def stages(sends, nd, nb, nh, rows, cols, weights, *refs):
    if weights:
        (q, k, v, g, seg_in, allow_in, x_in, q_out, k_out, v_out, w_out,
         qb, gb, kv, bias, pv, pk, rv, rk, ownv, ownk, seg, allow, x, xt, xall, vg, ws, wr,
         ls, ys, yr, fs, fr, ps, pr, xs, xr, zs, zr, cs, cr, hs, hr, hx, hy) = refs
    else:
        (q, k, v, g, seg_in, allow_in, q_out, k_out, v_out,
         qb, gb, kv, bias, pv, pk, rv, rk, ownv, ownk, seg, allow,
         ls, ys, yr, fs, fr, ps, pr) = refs
    d, b, u = lax.axis_index("dp"), lax.axis_index("blk"), lax.axis_index("uly")
    other = 1 - u
    half = rows // 2
    core, side = lax.rem(b, 2), b // 2
    twin = {"blk": side * 2 + 1 - core}
    across = {"blk": (1 - side) * 2 + core}
    slot = 2 * d + core
    scale = DH ** (-0.5)
    width = GROUP * DH

    mine = pl.ds(pl.multiple_of(u * half, half), half)
    window_mine = pl.ds(pl.multiple_of(b * rows + u * half, half), half)
    window_other = pl.ds(pl.multiple_of(b * rows + other * half, half), half)
    to_y = {"uly": other}

    def head_cols(who, c, w):
        return pl.ds(pl.multiple_of((who * nh + c) * w, w), w)

    barrier = pltpu.get_barrier_semaphore()
    count = 1
    pl.semaphore_signal(barrier, inc=1, device_id={"uly": other}, device_id_type=MESH)
    for r in range(1, nb):
        pl.semaphore_signal(
            barrier, inc=1, device_id={"blk": lax.rem(b + r, nb)}, device_id_type=MESH)
        count += 1
    if weights:
        for r in range(1, nd):
            for tc in (core, 1 - core):
                pl.semaphore_signal(
                    barrier, inc=1,
                    device_id={"dp": lax.rem(d + r, nd), "blk": side * 2 + tc},
                    device_id_type=MESH)
                count += 1

    local = []

    def fetch(src, dst):
        cp = pltpu.make_async_copy(src, dst, ls.at[len(local)])
        cp.start()
        local.append(cp)

    fetch(seg_in, seg)
    fetch(allow_in, allow)
    for c in range(nh):
        fetch(k.at[:, head_cols(u, c, DH)], kv.at[c, 0, window_mine])
        fetch(v.at[:, head_cols(u, c, DH)], kv.at[c, 1, window_mine])
        fetch(q.at[:, head_cols(u, c, width)], qb.at[c, mine])
        fetch(g.at[:, head_cols(u, c, width)], gb.at[c, mine])
    if weights:
        fetch(x_in, x)
    pl.semaphore_wait(barrier, count)

    def copy(src, dst, s, r, to, goes=None, comes=None):
        cp = Send(pltpu.make_async_remote_copy(
            src_ref=src, dst_ref=dst, send_sem=s, recv_sem=r, device_id=to,
            device_id_type=MESH), goes, comes)
        sends.append(cp)
        return cp

    ky, qy = [], []
    for c in range(nh):
        for n, src in enumerate((k, v)):
            ky.append(copy(src.at[:, head_cols(other, c, DH)], kv.at[c, n, window_mine],
                           ys.at[c, n], yr.at[c, n], to_y))
    for c in range(nh):
        for n, (src, dst) in enumerate(((q, qb), (g, gb))):
            qy.append(copy(src.at[:, head_cols(other, c, width)], dst.at[c, mine],
                           ys.at[c, 2 + n], yr.at[c, 2 + n], to_y))
    for c in range(nh):
        for cp in (ky[2 * c], ky[2 * c + 1], qy[2 * c], qy[2 * c + 1]):
            cp.start()

    fwd = [[] for _ in range(nh)]
    for c in range(nh):
        for r in range(1, nb):
            for n, src in enumerate((k, v)):
                cp = copy(src.at[:, head_cols(u, c, DH)], kv.at[c, n, window_mine],
                          fs.at[c, r, n], fr.at[c, r, n], {"blk": lax.rem(b + r, nb)},
                          b + r < nb, b >= r)
                cp.start()
                fwd[c].append(cp)
    def my_rows(who):
        return pl.ds(pl.multiple_of(who * rows, rows), rows)

    def column_rows(td, part, tc):
        return pl.ds(pl.multiple_of((td * nb + 2 * part + tc) * cols, 16), cols)

    def forward_kv(c):
        ky[2 * c].wait_recv()
        ky[2 * c + 1].wait_recv()
        for r in range(1, nb):
            cp = copy(kv.at[c, :, window_other], kv.at[c, :, window_other],
                      fs.at[c, r, 2], fr.at[c, r, 2], {"blk": lax.rem(b + r, nb)},
                      b + r < nb, b >= r)
            cp.start()
            fwd[c].append(cp)

    for cp in local:
        cp.wait()
    for j in range(1, nb):
        @pl.when(j > b)
        def _():
            kv[:, :, j * rows:(j + 1) * rows, :] = jnp.zeros((nh, 2, rows, DH), jnp.bfloat16)

        @pl.when(b >= j)
        def _():
            rv[:, j] = jnp.zeros((nh, rows, DH), jnp.bfloat16)
            rk[:, j] = jnp.zeros((nh, rows, DH), jnp.bfloat16)
    yield 'barrier'
    forward_kv(0)

    xtwin, xfar = [], [[] for _ in range(nd)]
    if weights:
        for t in range(xt.shape[0] // 128):
            xt[t * 128:(t + 1) * 128, :] = x[:, t * 128:(t + 1) * 128].T
        for r in range(1, nd):
            td = lax.rem(d + r, nd)
            for n, tc in enumerate((core, 1 - core)):
                cp = copy(xt.at[column_rows(td, u, tc)],
                          xall.at[u, :, my_rows(slot)],
                          xs.at[r, n], xr.at[r, n],
                          {"dp": td, "blk": side * 2 + tc})
                cp.start()
                xfar[r].append(cp)
        for part in range(2):
            cp = copy(xt.at[column_rows(d, part, 1 - core)], xall.at[part, :, my_rows(slot)],
                      xs.at[0, part], xr.at[0, part], twin)
            cp.start()
            xtwin.append(cp)
            xall[part, :, my_rows(slot)] = xt[column_rows(d, part, core), :]
    yield 'xt'
    for c in range(1, nh):
        forward_kv(c)
    yield 'fwd'
    i0 = lax.broadcasted_iota(jnp.int32, (rows, rows), 0)
    i1 = lax.broadcasted_iota(jnp.int32, (rows, rows), 1)
    seg_p = seg[:, pl.ds(pl.multiple_of(b * rows, rows), rows)]
    lane = lax.broadcasted_iota(jnp.int32, (1, nb), 1)
    table = allow[...]
    for j in range(nb):
        seg_j = jnp.broadcast_to(seg[:, j * rows:(j + 1) * rows], (rows, rows))
        seg_t = jnp.sum(jnp.where(i0 == i1, seg_j, 0), axis=1, keepdims=True)
        step = lax.rem(b - j + nb, nb)
        ok = jnp.sum(jnp.where(lane == step, table, 0), axis=1, keepdims=True)
        seen = (j * rows + i0 <= b * rows + i1) & (seg_t == seg_p) & (ok == 1)
        bias[j * rows:(j + 1) * rows, :] = jnp.where(seen, 0.0, NEG)

    yield 'mask'

    def four(ref, c):
        return jnp.concatenate(
            [ref[c, :, h * DH:(h + 1) * DH] for h in range(GROUP)], axis=0)

    parts_v, parts_k, far, partial = [], [], [], []
    near = [[] for _ in range(nh)]

    def send_parts(c, n, out, stage, land, own, keep):
        for j in range(nb):
            stage[c, j] = out[j * rows:(j + 1) * rows].astype(jnp.bfloat16)
        own[c] = stage[c, b].astype(jnp.float32)
        copies = []
        for r in range(1, nb):
            to = lax.rem(b + r, nb)
            cp = copy(stage.at[c, to], land.at[c, r], ps.at[n, c, r], pr.at[n, c, r],
                      {"blk": to}, b + r >= nb, b < r)
            cp.start()
            copies.append(cp)
        keep.append(copies)

    def total(c, copies, land, own):
        for cp in copies[c]:
            cp.wait_recv()
        acc = own[c]
        for r in range(1, nb):
            acc = acc + land[c, r].astype(jnp.float32)
        return acc.astype(jnp.bfloat16)

    def part_one(c):
        for cp in fwd[c]:
            cp.wait_recv()
        qy[2 * c].wait_recv()
        qy[2 * c + 1].wait_recv()
        scores = dot(kv[c, 0], four(qb, c), 1, 1) * scale
        hidden = bias[...]
        scores = scores + jnp.concatenate([hidden] * GROUP, axis=1)
        peak = jnp.max(scores, axis=0, keepdims=True)
        e = jnp.exp(scores - peak)
        probs = e * (1.0 / jnp.sum(e, axis=0, keepdims=True))
        low = probs.astype(jnp.bfloat16)
        send_parts(c, 0, dot(low, four(gb, c), 1, 0), pv, rv, ownv, parts_v)
        return probs, low

    def part_two(c, probs, low):
        grad = dot(kv[c, 1], four(gb, c), 1, 1)
        delta = jnp.sum(low.astype(jnp.float32) * grad, axis=0, keepdims=True)
        ds = (probs * (grad - delta)).astype(jnp.bfloat16)
        send_parts(c, 1, dot(ds, four(qb, c), 1, 0) * scale, pk, rk, ownk, parts_k)
        return ds

    def part_three(c, ds):
        dq = dot(kv[c, 0], ds, 0, 0) * scale
        for h in range(GROUP):
            at = c * width + h * DH
            q_out[:, at:at + DH] = dq[:, h * DH:(h + 1) * DH].T.astype(jnp.bfloat16)

    def to_twin(c, n, who):
        cp = copy(vg.at[c, my_rows(who)], vg.at[c, my_rows(who)], cs.at[c, n], cr.at[c, n], twin)
        cp.start()
        near[c].append(cp)

    def finish_v(c):
        low = total(c, parts_v, rv, ownv)
        v_out[:, c * DH:(c + 1) * DH] = low
        if weights:
            vg[c, my_rows(slot), :] = low
            for r in range(1, nd):
                cp = copy(vg.at[c, my_rows(slot)], vg.at[c, my_rows(slot)],
                          zs.at[c, r], zr.at[c, r], {"dp": lax.rem(d + r, nd)})
                cp.start()
                far.append(cp)
            to_twin(c, 0, slot)

    def forward(c):
        for r in range(1, nd):
            far[c * (nd - 1) + r - 1].wait_recv()
            to_twin(c, r, 2 * lax.rem(d - r + nd, nd) + core)

    def product(c):
        for cp in near[c]:
            cp.wait_recv()
        ws[c] = dot(xall[1 - side], vg[c], 1, 0).astype(jnp.bfloat16)
        cp = copy(ws.at[c], wr.at[c], hs.at[c], hr.at[c], across)
        cp.start()
        partial.append(cp)
        w_out[:, c * DH:(c + 1) * DH] = dot(xall[side], vg[c], 1, 0)

    shared = []

    def share(r):
        if weights and r < nd:
            for cp in xfar[r]:
                cp.wait_recv()
            pair = pl.ds(pl.multiple_of(2 * lax.rem(d - r + nd, nd) * rows, 2 * rows), 2 * rows)
            cp = copy(xall.at[u, :, pair], xall.at[u, :, pair], hx.at[r], hy.at[r], to_y)
            cp.start()
            shared.append(cp)

    state = part_one(0)
    yield 'one0'
    grads = [part_two(0, *state)]
    share(1)
    yield 'two0'
    for c in range(1, nh):
        state = part_one(c)
        yield 'one1'
        finish_v(c - 1)
        share(c + 1)
        grads.append(part_two(c, *state))
        yield 'two1'
    finish_v(nh - 1)
    for r in range(nh + 1, nd):
        share(r)
    yield 'finish1'
    for c in range(nh):
        part_three(c, grads[c])
    if weights:
        for c in range(nh - 1):
            forward(c)
    yield 'forward0'
    if weights:
        for cp in shared + xtwin:
            cp.wait_recv()
        for c in range(nh - 1):
            product(c)
    yield 'product0'
    for c in range(nh):
        k_out[:, c * DH:(c + 1) * DH] = total(c, parts_k, rk, ownk)
    yield 'kout'
    if weights:
        forward(nh - 1)
        yield 'forward1'
        product(nh - 1)
        for c in range(nh):
            partial[c].wait_recv()
            w_out[:, c * DH:(c + 1) * DH] += wr[c].astype(jnp.float32)


def emit(*refs):
    n = len(refs) // 2
    copies = [pltpu.make_async_copy(refs[t], refs[n + t], refs[-1].at[t]) for t in range(n)]
    for cp in copies:
        cp.start()
    for cp in copies:
        cp.wait()


def shards(query_act, key_act, value_act, out_grad, layer_input, segments, allow_table):
    nd, nb, nu = lax.axis_size("dp"), lax.axis_size("blk"), lax.axis_size("uly")
    half, qw = query_act.shape[1:]
    rows = half * nu
    kw = key_act.shape[2] // nu
    qw = qw // nu
    nh = kw // DH
    window = rows * nb
    din = layer_input.shape[2]
    cols = din // (nd * nb)
    weights = cols % 16 == 0 and nb == 4 and nd <= 8 and nu == 2
    bf, f32, sem = jnp.bfloat16, jnp.float32, pltpu.SemaphoreType.DMA
    vm = pltpu.VMEM
    scratch = [
        vm((nh, rows, GROUP * DH), bf), vm((nh, rows, GROUP * DH), bf),
        vm((nh, 2, window, DH), bf), vm((window, rows), f32),
        vm((nh, nb, rows, DH), bf), vm((nh, nb, rows, DH), bf),
        vm((nh, nb, rows, DH), bf), vm((nh, nb, rows, DH), bf),
        vm((nh, rows, DH), f32), vm((nh, rows, DH), f32),
        vm(segments.shape, jnp.int32), vm(allow_table.shape[1:], jnp.int32),
    ]
    sems = [sem((4 * nh + 3,)), sem((nh, 4)), sem((nh, 4)), sem((nh, nb, 3)), sem((nh, nb, 3)),
            sem((2, nh, nb)), sem((2, nh, nb))]
    outs = [jax.ShapeDtypeStruct((rows, qw), bf), jax.ShapeDtypeStruct((rows, kw), bf),
            jax.ShapeDtypeStruct((rows, kw), bf)]
    args = [query_act[0], key_act[0], value_act[0], out_grad[0], segments, allow_table[0]]
    if weights:
        args.append(layer_input[0])
        outs.append(jax.ShapeDtypeStruct((cols, kw), f32))
        scratch += [vm((rows, din), bf), vm((din, rows), bf), vm((2, cols, nd * 2 * rows), bf),
                    vm((nh, nd * 2 * rows, DH), bf), vm((nh, cols, DH), bf),
                    vm((nh, cols, DH), bf)]
        sems += [sem((nd, 2)), sem((nd, 2)), sem((nh, nd)), sem((nh, nd)),
                 sem((nh, nd)), sem((nh, nd)), sem((nh,)), sem((nh,)),
                 sem((nd,)), sem((nd,))]
    spec = pl.BlockSpec(memory_space=pltpu.VMEM)
    res = pl.pallas_call(
        functools.partial(kernel, CUT, nd, nb, nh, rows, cols, weights),
        out_shape=outs,
        in_specs=[pl.BlockSpec(memory_space=pltpu.HBM)] * len(args),
        out_specs=[spec] * len(outs),
        scratch_shapes=scratch + sems,
        compiler_params=pltpu.CompilerParams(
            collective_id=0, has_side_effects=True, vmem_limit_bytes=52_000_000),
    )(*[pltpu.with_memory_space_constraint(a, pltpu.HBM) for a in args])
    res = pl.pallas_call(
        emit,
        out_shape=outs,
        in_specs=[spec] * len(outs),
        out_specs=[pl.BlockSpec(memory_space=pltpu.HBM)] * len(outs),
        scratch_shapes=[sem((len(outs),))],
        compiler_params=pltpu.CompilerParams(vmem_limit_bytes=2 * 1024 * 1024),
    )(*res)
    if weights:
        weight_out = res[3]
    else:
        weight_out = lax.psum_scatter(
            dot(layer_input[0], res[2], 0, 0), ("dp", "blk"), scatter_dimension=0, tiled=True)
    return (res[0][None], res[1][None], res[2][None], weight_out)


def solution(mesh):
    return jax.shard_map(
        shards,
        mesh=mesh,
        in_specs=(
            P("dp", ("blk", "uly"), None),
            P("dp", ("blk", "uly"), None),
            P("dp", ("blk", "uly"), None),
            P("dp", ("blk", "uly"), None),
            P("dp", "blk", None),
            P("dp", None),
            P("dp", "blk", None),
        ),
        out_specs=(
            P("dp", "blk", "uly"),
            P("dp", "blk", "uly"),
            P("dp", "blk", "uly"),
            P(("dp", "blk"), "uly"),
        ),
        check_vma=False,
    )
```

```python
import functools

import jax
import jax.numpy as jnp
from jax import lax
from jax.experimental import pallas as pl
from jax.experimental.pallas import tpu as pltpu
from jax.sharding import PartitionSpec as P

DH = 128
GROUP = 4
MESH = pl.DeviceIdType.MESH
NEG = -1e30
CUT = None


def dot(a, b, ca, cb):
    return lax.dot_general(a, b, (((ca,), (cb,)), ((), ())), preferred_element_type=jnp.float32)


def guarded(cond, run):
    if cond is None:
        run()
    else:
        pl.when(cond)(run)


class Send:
    def __init__(self, cp, goes, comes):
        self.cp, self.goes, self.comes = cp, goes, comes
        self.started, self.landed = False, False

    def start(self):
        self.started = True
        guarded(self.goes, self.cp.start)

    def wait_recv(self):
        if self.started and not self.landed:
            self.landed = True
            guarded(self.comes, self.cp.wait_recv)

    def finish(self):
        if self.started:
            self.wait_recv()
            guarded(self.goes, self.cp.wait_send)


def kernel(cut, *args):
    sends = []
    for name in stages(sends, *args):
        if name == cut:
            break
    for cp in sends:
        cp.finish()


def stages(sends, nd, nb, nh, rows, cols, weights, *refs):
    if weights:
        (q, k, v, g, seg_in, allow_in, x_in, q_out, k_out, v_out, w_out,
         qb, gb, kv, bias, pv, pk, rv, rk, ownv, ownk, seg, allow, x, xt, xall, vg, ws, wr,
         ls, ys, yr, fs, fr, ps, pr, xs, xr, zs, zr, cs, cr, hs, hr, hx, hy) = refs
    else:
        (q, k, v, g, seg_in, allow_in, q_out, k_out, v_out,
         qb, gb, kv, bias, pv, pk, rv, rk, ownv, ownk, seg, allow,
         ls, ys, yr, fs, fr, ps, pr) = refs
    d, b, u = lax.axis_index("dp"), lax.axis_index("blk"), lax.axis_index("uly")
    other = 1 - u
    half = rows // 2
    core, side = lax.rem(b, 2), b // 2
    twin = {"blk": side * 2 + 1 - core}
    across = {"blk": (1 - side) * 2 + core}
    slot = 2 * d + core
    scale = DH ** (-0.5)
    width = GROUP * DH

    mine = pl.ds(pl.multiple_of(u * half, half), half)
    window_mine = pl.ds(pl.multiple_of(b * rows + u * half, half), half)
    window_other = pl.ds(pl.multiple_of(b * rows + other * half, half), half)
    to_y = {"uly": other}

    def head_cols(who, c, w):
        return pl.ds(pl.multiple_of((who * nh + c) * w, w), w)

    barrier = pltpu.get_barrier_semaphore()
    count = 1
    pl.semaphore_signal(barrier, inc=1, device_id={"uly": other}, device_id_type=MESH)
    for r in range(1, nb):
        pl.semaphore_signal(
            barrier, inc=1, device_id={"blk": lax.rem(b + r, nb)}, device_id_type=MESH)
        count += 1
    if weights:
        for r in range(1, nd):
            for tc in (core, 1 - core):
                pl.semaphore_signal(
                    barrier, inc=1,
                    device_id={"dp": lax.rem(d + r, nd), "blk": side * 2 + tc},
                    device_id_type=MESH)
                count += 1

    local = []

    def fetch(src, dst):
        cp = pltpu.make_async_copy(src, dst, ls.at[len(local)])
        cp.start()
        local.append(cp)

    fetch(seg_in, seg)
    fetch(allow_in, allow)
    for c in range(nh):
        fetch(k.at[:, head_cols(u, c, DH)], kv.at[c, 0, window_mine])
        fetch(v.at[:, head_cols(u, c, DH)], kv.at[c, 1, window_mine])
        fetch(q.at[:, head_cols(u, c, width)], qb.at[c, mine])
        fetch(g.at[:, head_cols(u, c, width)], gb.at[c, mine])
    if weights:
        fetch(x_in, x)
    pl.semaphore_wait(barrier, count)

    def copy(src, dst, s, r, to, goes=None, comes=None):
        cp = Send(pltpu.make_async_remote_copy(
            src_ref=src, dst_ref=dst, send_sem=s, recv_sem=r, device_id=to,
            device_id_type=MESH), goes, comes)
        sends.append(cp)
        return cp

    ky, qy = [], []
    for c in range(nh):
        for n, src in enumerate((k, v)):
            ky.append(copy(src.at[:, head_cols(other, c, DH)], kv.at[c, n, window_mine],
                           ys.at[c, n], yr.at[c, n], to_y))
    for c in range(nh):
        for n, (src, dst) in enumerate(((q, qb), (g, gb))):
            qy.append(copy(src.at[:, head_cols(other, c, width)], dst.at[c, mine],
                           ys.at[c, 2 + n], yr.at[c, 2 + n], to_y))
    for c in range(nh):
        for cp in (ky[2 * c], ky[2 * c + 1], qy[2 * c], qy[2 * c + 1]):
            cp.start()

    fwd = [[] for _ in range(nh)]
    for c in range(nh):
        for r in range(1, nb):
            for n, src in enumerate((k, v)):
                cp = copy(src.at[:, head_cols(u, c, DH)], kv.at[c, n, window_mine],
                          fs.at[c, r, n], fr.at[c, r, n], {"blk": lax.rem(b + r, nb)},
                          b + r < nb, b >= r)
                cp.start()
                fwd[c].append(cp)
    def my_rows(who):
        return pl.ds(pl.multiple_of(who * rows, rows), rows)

    def column_rows(td, part, tc):
        return pl.ds(pl.multiple_of((td * nb + 2 * part + tc) * cols, 16), cols)

    def forward_kv(c):
        ky[2 * c].wait_recv()
        ky[2 * c + 1].wait_recv()
        for r in range(1, nb):
            cp = copy(kv.at[c, :, window_other], kv.at[c, :, window_other],
                      fs.at[c, r, 2], fr.at[c, r, 2], {"blk": lax.rem(b + r, nb)},
                      b + r < nb, b >= r)
            cp.start()
            fwd[c].append(cp)

    xtwin, xfar = [], [[] for _ in range(nd)]
    if weights:
        local.pop().wait()
        for t in range(xt.shape[0] // 128):
            xt[t * 128:(t + 1) * 128, :] = x[:, t * 128:(t + 1) * 128].T
        for r in range(1, nd):
            td = lax.rem(d + r, nd)
            for n, tc in enumerate((core, 1 - core)):
                cp = copy(xt.at[column_rows(td, u, tc)],
                          xall.at[u, :, my_rows(slot)],
                          xs.at[r, n], xr.at[r, n],
                          {"dp": td, "blk": side * 2 + tc})
                cp.start()
                xfar[r].append(cp)
        for part in range(2):
            cp = copy(xt.at[column_rows(d, part, 1 - core)], xall.at[part, :, my_rows(slot)],
                      xs.at[0, part], xr.at[0, part], twin)
            cp.start()
            xtwin.append(cp)
            xall[part, :, my_rows(slot)] = xt[column_rows(d, part, core), :]
    for cp in local:
        cp.wait()
    for j in range(1, nb):
        @pl.when(j > b)
        def _():
            kv[:, :, j * rows:(j + 1) * rows, :] = jnp.zeros((nh, 2, rows, DH), jnp.bfloat16)

        @pl.when(b >= j)
        def _():
            rv[:, j] = jnp.zeros((nh, rows, DH), jnp.bfloat16)
            rk[:, j] = jnp.zeros((nh, rows, DH), jnp.bfloat16)
    yield 'barrier'
    forward_kv(0)

    yield 'xt'
    for c in range(1, nh):
        forward_kv(c)
    yield 'fwd'
    i0 = lax.broadcasted_iota(jnp.int32, (rows, rows), 0)
    i1 = lax.broadcasted_iota(jnp.int32, (rows, rows), 1)
    seg_p = seg[:, pl.ds(pl.multiple_of(b * rows, rows), rows)]
    lane = lax.broadcasted_iota(jnp.int32, (1, nb), 1)
    table = allow[...]
    for j in range(nb):
        seg_j = jnp.broadcast_to(seg[:, j * rows:(j + 1) * rows], (rows, rows))
        seg_t = jnp.sum(jnp.where(i0 == i1, seg_j, 0), axis=1, keepdims=True)
        step = lax.rem(b - j + nb, nb)
        ok = jnp.sum(jnp.where(lane == step, table, 0), axis=1, keepdims=True)
        seen = (j * rows + i0 <= b * rows + i1) & (seg_t == seg_p) & (ok == 1)
        bias[j * rows:(j + 1) * rows, :] = jnp.where(seen, 0.0, NEG)

    yield 'mask'

    def four(ref, c):
        return jnp.concatenate(
            [ref[c, :, h * DH:(h + 1) * DH] for h in range(GROUP)], axis=0)

    parts_v, parts_k, far, partial = [], [], [], []
    near = [[] for _ in range(nh)]

    def send_parts(c, n, out, stage, land, own, keep):
        for j in range(nb):
            stage[c, j] = out[j * rows:(j + 1) * rows].astype(jnp.bfloat16)
        own[c] = stage[c, b].astype(jnp.float32)
        copies = []
        for r in range(1, nb):
            to = lax.rem(b + r, nb)
            cp = copy(stage.at[c, to], land.at[c, r], ps.at[n, c, r], pr.at[n, c, r],
                      {"blk": to}, b + r >= nb, b < r)
            cp.start()
            copies.append(cp)
        keep.append(copies)

    def total(c, copies, land, own):
        for cp in copies[c]:
            cp.wait_recv()
        acc = own[c]
        for r in range(1, nb):
            acc = acc + land[c, r].astype(jnp.float32)
        return acc.astype(jnp.bfloat16)

    def part_one(c):
        for cp in fwd[c]:
            cp.wait_recv()
        qy[2 * c].wait_recv()
        scores = dot(kv[c, 0], four(qb, c), 1, 1) * scale
        hidden = bias[...]
        scores = scores + jnp.concatenate([hidden] * GROUP, axis=1)
        peak = jnp.max(scores, axis=0, keepdims=True)
        e = jnp.exp(scores - peak)
        probs = e * (1.0 / jnp.sum(e, axis=0, keepdims=True))
        low = probs.astype(jnp.bfloat16)
        qy[2 * c + 1].wait_recv()
        send_parts(c, 0, dot(low, four(gb, c), 1, 0), pv, rv, ownv, parts_v)
        return probs, low

    def part_two(c, probs, low):
        grad = dot(kv[c, 1], four(gb, c), 1, 1)
        delta = jnp.sum(low.astype(jnp.float32) * grad, axis=0, keepdims=True)
        ds = (probs * (grad - delta)).astype(jnp.bfloat16)
        send_parts(c, 1, dot(ds, four(qb, c), 1, 0) * scale, pk, rk, ownk, parts_k)
        return ds

    def part_three(c, ds):
        dq = dot(kv[c, 0], ds, 0, 0) * scale
        for h in range(GROUP):
            at = c * width + h * DH
            q_out[:, at:at + DH] = dq[:, h * DH:(h + 1) * DH].T.astype(jnp.bfloat16)

    def to_twin(c, n, who):
        cp = copy(vg.at[c, my_rows(who)], vg.at[c, my_rows(who)], cs.at[c, n], cr.at[c, n], twin)
        cp.start()
        near[c].append(cp)

    def finish_v(c):
        low = total(c, parts_v, rv, ownv)
        v_out[:, c * DH:(c + 1) * DH] = low
        if weights:
            vg[c, my_rows(slot), :] = low
            for r in range(1, nd):
                cp = copy(vg.at[c, my_rows(slot)], vg.at[c, my_rows(slot)],
                          zs.at[c, r], zr.at[c, r], {"dp": lax.rem(d + r, nd)})
                cp.start()
                far.append(cp)
            to_twin(c, 0, slot)

    def forward(c):
        for r in range(1, nd):
            far[c * (nd - 1) + r - 1].wait_recv()
            to_twin(c, r, 2 * lax.rem(d - r + nd, nd) + core)

    def product(c):
        for cp in near[c]:
            cp.wait_recv()
        ws[c] = dot(xall[1 - side], vg[c], 1, 0).astype(jnp.bfloat16)
        cp = copy(ws.at[c], wr.at[c], hs.at[c], hr.at[c], across)
        cp.start()
        partial.append(cp)
        w_out[:, c * DH:(c + 1) * DH] = dot(xall[side], vg[c], 1, 0)

    shared = []

    def share(r):
        if weights and r < nd:
            for cp in xfar[r]:
                cp.wait_recv()
            pair = pl.ds(pl.multiple_of(2 * lax.rem(d - r + nd, nd) * rows, 2 * rows), 2 * rows)
            cp = copy(xall.at[u, :, pair], xall.at[u, :, pair], hx.at[r], hy.at[r], to_y)
            cp.start()
            shared.append(cp)

    state = part_one(0)
    yield 'one0'
    grads = [part_two(0, *state)]
    share(1)
    yield 'two0'
    for c in range(1, nh):
        state = part_one(c)
        yield 'one1'
        finish_v(c - 1)
        share(c + 1)
        grads.append(part_two(c, *state))
        yield 'two1'
    finish_v(nh - 1)
    for r in range(nh + 1, nd):
        share(r)
    yield 'finish1'
    for c in range(nh):
        part_three(c, grads[c])
    if weights:
        for c in range(nh - 1):
            forward(c)
    yield 'forward0'
    if weights:
        for cp in shared + xtwin:
            cp.wait_recv()
        for c in range(nh - 1):
            product(c)
    yield 'product0'
    for c in range(nh):
        k_out[:, c * DH:(c + 1) * DH] = total(c, parts_k, rk, ownk)
    yield 'kout'
    if weights:
        forward(nh - 1)
        yield 'forward1'
        product(nh - 1)
        for c in range(nh):
            partial[c].wait_recv()
            w_out[:, c * DH:(c + 1) * DH] += wr[c].astype(jnp.float32)


def emit(*refs):
    n = len(refs) // 2
    copies = [pltpu.make_async_copy(refs[t], refs[n + t], refs[-1].at[t]) for t in range(n)]
    for cp in copies:
        cp.start()
    for cp in copies:
        cp.wait()


def shards(query_act, key_act, value_act, out_grad, layer_input, segments, allow_table):
    nd, nb, nu = lax.axis_size("dp"), lax.axis_size("blk"), lax.axis_size("uly")
    half, qw = query_act.shape[1:]
    rows = half * nu
    kw = key_act.shape[2] // nu
    qw = qw // nu
    nh = kw // DH
    window = rows * nb
    din = layer_input.shape[2]
    cols = din // (nd * nb)
    weights = cols % 16 == 0 and nb == 4 and nd <= 8 and nu == 2
    bf, f32, sem = jnp.bfloat16, jnp.float32, pltpu.SemaphoreType.DMA
    vm = pltpu.VMEM
    scratch = [
        vm((nh, rows, GROUP * DH), bf), vm((nh, rows, GROUP * DH), bf),
        vm((nh, 2, window, DH), bf), vm((window, rows), f32),
        vm((nh, nb, rows, DH), bf), vm((nh, nb, rows, DH), bf),
        vm((nh, nb, rows, DH), bf), vm((nh, nb, rows, DH), bf),
        vm((nh, rows, DH), f32), vm((nh, rows, DH), f32),
        vm(segments.shape, jnp.int32), vm(allow_table.shape[1:], jnp.int32),
    ]
    sems = [sem((4 * nh + 3,)), sem((nh, 4)), sem((nh, 4)), sem((nh, nb, 3)), sem((nh, nb, 3)),
            sem((2, nh, nb)), sem((2, nh, nb))]
    outs = [jax.ShapeDtypeStruct((rows, qw), bf), jax.ShapeDtypeStruct((rows, kw), bf),
            jax.ShapeDtypeStruct((rows, kw), bf)]
    args = [query_act[0], key_act[0], value_act[0], out_grad[0], segments, allow_table[0]]
    if weights:
        args.append(layer_input[0])
        outs.append(jax.ShapeDtypeStruct((cols, kw), f32))
        scratch += [vm((rows, din), bf), vm((din, rows), bf), vm((2, cols, nd * 2 * rows), bf),
                    vm((nh, nd * 2 * rows, DH), bf), vm((nh, cols, DH), bf),
                    vm((nh, cols, DH), bf)]
        sems += [sem((nd, 2)), sem((nd, 2)), sem((nh, nd)), sem((nh, nd)),
                 sem((nh, nd)), sem((nh, nd)), sem((nh,)), sem((nh,)),
                 sem((nd,)), sem((nd,))]
    spec = pl.BlockSpec(memory_space=pltpu.VMEM)
    res = pl.pallas_call(
        functools.partial(kernel, CUT, nd, nb, nh, rows, cols, weights),
        out_shape=outs,
        in_specs=[pl.BlockSpec(memory_space=pltpu.HBM)] * len(args),
        out_specs=[spec] * len(outs),
        scratch_shapes=scratch + sems,
        compiler_params=pltpu.CompilerParams(
            collective_id=0, has_side_effects=True, vmem_limit_bytes=52_000_000),
    )(*[pltpu.with_memory_space_constraint(a, pltpu.HBM) for a in args])
    res = pl.pallas_call(
        emit,
        out_shape=outs,
        in_specs=[spec] * len(outs),
        out_specs=[pl.BlockSpec(memory_space=pltpu.HBM)] * len(outs),
        scratch_shapes=[sem((len(outs),))],
        compiler_params=pltpu.CompilerParams(vmem_limit_bytes=2 * 1024 * 1024),
    )(*res)
    if weights:
        weight_out = res[3]
    else:
        weight_out = lax.psum_scatter(
            dot(layer_input[0], res[2], 0, 0), ("dp", "blk"), scatter_dimension=0, tiled=True)
    return (res[0][None], res[1][None], res[2][None], weight_out)


def solution(mesh):
    return jax.shard_map(
        shards,
        mesh=mesh,
        in_specs=(
            P("dp", ("blk", "uly"), None),
            P("dp", ("blk", "uly"), None),
            P("dp", ("blk", "uly"), None),
            P("dp", ("blk", "uly"), None),
            P("dp", "blk", None),
            P("dp", None),
            P("dp", "blk", None),
        ),
        out_specs=(
            P("dp", "blk", "uly"),
            P("dp", "blk", "uly"),
            P("dp", "blk", "uly"),
            P(("dp", "blk"), "uly"),
        ),
        check_vma=False,
    )
```
